32 devices in a mesh: wide: 8 (over y, x, core), narrow: 4 (over z).
Axes of the slice: x: 2, y: 2, z: 4, core: 2. Of those that a mesh axis runs over, the one named last changes fastest.
Arguments:
- query_tokens: bfloat16 [4096, 768], P(('wide', 'narrow')), may hold values from -6 to 6
- passage_tokens: bfloat16 [12288, 768], P(('wide', 'narrow')), may hold values from -6 to 6
- query_cotangent: bfloat16 [4096, 768], P(('wide', 'narrow')), may hold values from -6 to 6
- passage_cotangent: bfloat16 [12288, 768], P(('wide', 'narrow')), may hold values from -6 to 6
- query_segments: int32 [8, 512], P('wide'), may hold values from -1 to 15, as said below
- passage_segments: int32 [24, 512], P('wide'), may hold values from -1 to 3, as said below
- query_cls: int32 [8, 16], P('wide'), may hold values from 0 to 485, as said below
- passage_cls: int32 [24, 4], P('wide'), may hold values from 0 to 485, as said below
- query_weight: bfloat16 [2, 768, 768], P(None, None, 'narrow'), may hold values from -0.3125 to 0.3125
- query_bias: float32 [2, 768], P(None, 'narrow'), may hold values from -3 to 3
- key_weight: bfloat16 [2, 768, 768], P(None, None, 'narrow'), may hold values from -0.3125 to 0.3125
- value_weight: bfloat16 [2, 768, 768], P(None, None, 'narrow'), may hold values from -0.21875 to 0.21875
- value_bias: float32 [2, 768], P(None, 'narrow'), may hold values from -3 to 3
- out_weight: bfloat16 [2, 768, 768], P(None, 'narrow'), may hold values from -1.25 to 1.25
- out_bias: float32 [2, 768], replicated, may hold values from -3 to 3
- norm1_gain: float32 [2, 768], replicated, may hold values from 0.25 to 1.75
- norm1_bias: float32 [2, 768], replicated, may hold values from -3 to 3
- inner_weight: bfloat16 [2, 768, 3072], P(None, None, 'narrow'), may hold values from -0.21875 to 0.21875
- inner_bias: float32 [2, 3072], P(None, 'narrow'), may hold values from -3 to 3
- outer_weight: bfloat16 [2, 3072, 768], P(None, 'narrow'), may hold values from -0.109375 to 0.109375
- outer_bias: float32 [2, 768], replicated, may hold values from -3 to 3
- norm2_gain: float32 [2, 768], replicated, may hold values from 0.25 to 1.75
- norm2_bias: float32 [2, 768], replicated, may hold values from -3 to 3
Outputs:
- query_out: bfloat16 [4096, 768], P(('wide', 'narrow'))
- passage_out: bfloat16 [12288, 768], P(('wide', 'narrow'))
- query_grad_in: bfloat16 [4096, 768], P(('wide', 'narrow'))
- passage_grad_in: bfloat16 [12288, 768], P(('wide', 'narrow'))
- query_pooled: bfloat16 [8, 16, 768], P('wide', None, 'narrow')
- passage_pooled: bfloat16 [24, 4, 768], P('wide', None, 'narrow')
- grad_query_weight: float32 [2, 768, 768], P(None, None, 'narrow')
- grad_query_bias: float32 [2, 768], P(None, 'narrow')
- grad_key_weight: float32 [2, 768, 768], P(None, None, 'narrow')
- grad_value_weight: float32 [2, 768, 768], P(None, None, 'narrow')
- grad_value_bias: float32 [2, 768], P(None, 'narrow')
- grad_out_weight: float32 [2, 768, 768], P(None, 'narrow')
- grad_out_bias: float32 [2, 768], replicated
- grad_norm1_gain: float32 [2, 768], replicated
- grad_norm1_bias: float32 [2, 768], replicated
- grad_inner_weight: float32 [2, 768, 3072], P(None, None, 'narrow')
- grad_inner_bias: float32 [2, 3072], P(None, 'narrow')
- grad_outer_weight: float32 [2, 3072, 768], P(None, 'narrow')
- grad_outer_bias: float32 [2, 768], replicated
- grad_norm2_gain: float32 [2, 768], replicated
- grad_norm2_bias: float32 [2, 768], replicated
The draws below stay inside these ranges and needn't reach their ends.
Inputs may be any that keep to these rules, and one draw needn't show every extreme that they name: `query_segments`: segment numbers never fall along a row and rise by one from 0 at each segment's first token; every segment spans 2 or more tokens; -1 marks padding at the end of every row. `passage_segments`: as for query_segments. query_cls[r, j] is the first position of segment j in row r of query_segments. passage_cls[r, j] is the first position of segment j in row r of passage_segments.
All inputs are finite; a program needn't handle non-finite values.
Results may differ from the reference program's by a relative error of at most 0.018.
The reference program's roundings to bfloat16 on the way count: a program that leaves them out, or rounds other values in their place, can miss the bound.
Values may be sent and summed in bfloat16 or wider, within the bound.
No kernel may reach another device: no remote copies, remote signals or barrier semaphores. Data moves between devices by JAX's collectives and lax.ppermute only.
A program may use at most 128 MiB of HBM per device.

```python
import math
import jax
import jax.numpy as jnp
from jax import lax

D = 768
HEADS = 12
HDIM = 64
FF = 3072
LEN = 512
SEG_P = 4
SEG_Q = 16
P_ROWS = 24
Q_ROWS = 8
P_TOKENS = 12288
Q_TOKENS = 4096


def segment_layout(key, row_count, seg_count):
    filled = LEN - LEN // 20
    spare = filled - seg_count

    def one_row(row_key, row_number):
        shuffled = jax.random.permutation(row_key, spare - 1) + 1
        cut_points = jnp.sort(shuffled[:seg_count - 1]).astype(jnp.int32)
        last_cut = jnp.where(row_number == 0, spare - 1, cut_points[seg_count - 2]).astype(jnp.int32)
        cut_points = cut_points.at[seg_count - 2].set(last_cut)
        starts = jnp.concatenate([jnp.zeros((1,), jnp.int32), cut_points]) + jnp.arange(seg_count, dtype=jnp.int32)
        places = jnp.arange(LEN, dtype=jnp.int32)
        labels = jnp.sum((starts[None, :] <= places[:, None]).astype(jnp.int32), 1) - 1
        labels = jnp.where(places < filled, labels, -1).astype(jnp.int32)
        return (labels, starts)
    return jax.vmap(one_row)(jax.random.split(key, row_count), jnp.arange(row_count, dtype=jnp.int32))


def draw_query_segments(key, part):
    return segment_layout(jax.random.fold_in(key, 11), Q_ROWS, SEG_Q)[0]


def draw_query_cls(key, part):
    return segment_layout(jax.random.fold_in(key, 11), Q_ROWS, SEG_Q)[1]


def draw_passage_segments(key, part):
    return segment_layout(jax.random.fold_in(key, 12), P_ROWS, SEG_P)[0]


def draw_passage_cls(key, part):
    return segment_layout(jax.random.fold_in(key, 12), P_ROWS, SEG_P)[1]


def levels(key, shape, cuts, smallest, largest):
    loudness, own = 1.0, jax.random.fold_in(key, 6)
    for axis_at, blocks in cuts:
        steps = jnp.exp(jax.random.uniform(jax.random.fold_in(own, axis_at), (blocks,), jnp.float32, smallest / len(cuts), largest / len(cuts)))
        loudness = loudness * jnp.repeat(steps, shape[axis_at] // blocks).reshape([-1 if axis == axis_at else 1 for axis in range(len(shape))])
    return loudness


def gaussian(stream_key, dims, width, limit, cuts=(), held_as=jnp.bfloat16):
    factor_of = levels(stream_key, dims, cuts, -0.22, 0.18) if cuts else 1.0
    values = jax.random.normal(stream_key, dims, jnp.float32) * width * factor_of
    return jnp.minimum(jnp.maximum(values, -limit), limit).astype(held_as)


def setup_inputs(seed: int = 0) -> dict:
    keys = jax.random.split(jax.random.key(seed), 24)
    return {
        "query_tokens": gaussian(keys[0], (Q_TOKENS, D), 1.0, 6.0, ((0, 32),)),
        "passage_tokens": gaussian(keys[1], (P_TOKENS, D), 1.0, 6.0, ((0, 32),)),
        "query_cotangent": gaussian(keys[2], (Q_TOKENS, D), 1.0, 6.0, ((0, 32),)),
        "passage_cotangent": gaussian(keys[3], (P_TOKENS, D), 1.0, 6.0, ((0, 32),)),
        "query_segments": draw_query_segments(jax.random.fold_in(keys[23], 71), 0),
        "passage_segments": draw_passage_segments(jax.random.fold_in(keys[23], 71), 0),
        "query_cls": draw_query_cls(jax.random.fold_in(keys[23], 71), 0),
        "passage_cls": draw_passage_cls(jax.random.fold_in(keys[23], 71), 0),
        "query_weight": gaussian(keys[8], (2, D, D), (D // 2) ** -0.5, 0.3125, ((2, 4),)),
        "query_bias": gaussian(keys[9], (2, D), 0.5, 3.0, ((1, 4),), jnp.float32),
        "key_weight": gaussian(keys[10], (2, D, D), (D // 2) ** -0.5, 0.3125, ((2, 4),)),
        "value_weight": gaussian(keys[11], (2, D, D), D ** -0.5, 0.21875, ((2, 4),)),
        "value_bias": gaussian(keys[12], (2, D), 0.5, 3.0, ((1, 4),), jnp.float32),
        "out_weight": gaussian(keys[13], (2, D, D), (D // 32) ** -0.5, 1.25, ((1, 4),)),
        "out_bias": gaussian(keys[14], (2, D), 0.5, 3.0, (), jnp.float32),
        "norm1_gain": jnp.clip(1.0 + 0.15 * jax.random.normal(keys[15], (2, D), jnp.float32), 0.25, 1.75),
        "norm1_bias": gaussian(keys[16], (2, D), 0.5, 3.0, (), jnp.float32),
        "inner_weight": gaussian(keys[17], (2, D, FF), D ** -0.5, 0.21875, ((2, 4),)),
        "inner_bias": gaussian(keys[18], (2, FF), 0.5, 3.0, ((1, 4),), jnp.float32),
        "outer_weight": gaussian(keys[19], (2, FF, D), FF ** -0.5, 0.109375, ((1, 4),)),
        "outer_bias": gaussian(keys[20], (2, D), 0.5, 3.0, (), jnp.float32),
        "norm2_gain": jnp.clip(1.0 + 0.15 * jax.random.normal(keys[21], (2, D), jnp.float32), 0.25, 1.75),
        "norm2_bias": gaussian(keys[22], (2, D), 0.5, 3.0, (), jnp.float32),
    }


@jax.custom_vjp
def low(v):
    return lax.optimization_barrier(v.astype(jnp.bfloat16)).astype(jnp.float32)

@jax.custom_vjp
def low_back(v):
    return v

def low_keep(v):
    return (low(v), None)

def low_pass(kept, grad):
    return (grad,)

def back_keep(v):
    return (v, None)

def back_low(kept, grad):
    return (low(grad),)
low.defvjp(low_keep, low_pass)
low_back.defvjp(back_keep, back_low)
HIGHEST = lax.Precision.HIGHEST
NORM_EPS = 1e-05
MASKED = -1e+30

def matmul(left, right):
    return jnp.dot(left, right, precision=HIGHEST, preferred_element_type=jnp.float32)

def layer_norm(values, gain, bias):
    centred = values - lax.optimization_barrier(jnp.mean(values, -1, keepdims=True))
    variance = lax.optimization_barrier(jnp.mean(centred * centred, -1, keepdims=True))
    return centred * lax.rsqrt(variance + NORM_EPS) * gain + bias

def forward(inputs, labels, params):
    query_weight, query_bias, key_weight, value_weight, value_bias, out_weight, out_bias, norm1_gain, norm1_bias, inner_weight, inner_bias, outer_weight, outer_bias, norm2_gain, norm2_bias = params
    groups = inputs.shape[0]
    split_shape = (groups, LEN, HEADS, HDIM)
    flat = inputs.reshape(-1, D)
    queries = low(low_back(matmul(flat, query_weight) + query_bias)).reshape(split_shape)
    key_vecs = low(low_back(matmul(flat, key_weight))).reshape(split_shape)
    value_vecs = low(low_back(matmul(flat, value_weight) + value_bias)).reshape(split_shape)
    scores = low_back(jnp.einsum('gqhd,gkhd->ghqk', queries, key_vecs, precision=HIGHEST, preferred_element_type=jnp.float32) * HDIM ** (-0.5))
    allowed = ((labels[:, :, None] == labels[:, None, :]) & (labels[:, None, :] >= 0))[:, None]
    row_top = lax.optimization_barrier(jnp.max(jnp.where(allowed, scores, MASKED), -1, keepdims=True))
    unnorm = jnp.exp(jnp.where(allowed, scores - row_top, MASKED))
    totals = jnp.maximum(lax.optimization_barrier(jnp.sum(unnorm, -1, keepdims=True)), 1.0)
    probs = unnorm / totals
    attended = jnp.einsum('ghqk,gkhd->gqhd', low(probs), value_vecs, precision=HIGHEST, preferred_element_type=jnp.float32).reshape(-1, D)
    attended = low(low_back(attended))
    resid1 = flat + low_back(matmul(attended, out_weight)) + out_bias
    hidden1 = layer_norm(resid1, norm1_gain, norm1_bias)
    inner_pre = low_back(matmul(low(hidden1), inner_weight) + inner_bias)
    activated = low(jax.nn.gelu(inner_pre, approximate=False))
    resid2 = hidden1 + low_back(matmul(activated, outer_weight)) + outer_bias
    return layer_norm(resid2, norm2_gain, norm2_bias).reshape(groups, LEN, D)

def tower_reference(tokens, cotangent, labels, cls_pos, params):
    row_count = labels.shape[0]
    group = math.gcd(row_count, max(1, 4096 // LEN))
    steps_count = row_count // group
    inputs = tokens.astype(jnp.float32).reshape(steps_count, group, LEN, D)
    upstream = cotangent.astype(jnp.float32).reshape(steps_count, group, LEN, D)
    grouped_labels = labels.reshape(steps_count, group, LEN)
    zeros_tree = jax.tree.map(jnp.zeros_like, params)

    def step_fn(totals_tree, item):
        x_group, c_group, l_group = item
        result, pull = jax.vjp(lambda inputs_v, params_v: forward(inputs_v, l_group, params_v), x_group, params)
        grad_inputs, grad_params = pull(c_group)
        return (jax.tree.map(jnp.add, totals_tree, grad_params), (result.astype(jnp.bfloat16), grad_inputs.astype(jnp.bfloat16)))
    grads, (outputs, grad_in) = lax.scan(step_fn, zeros_tree, (inputs, upstream, grouped_labels))
    outputs = outputs.reshape(row_count, LEN, D)
    pooled = jax.vmap(lambda row_out, picks: row_out[picks])(outputs, cls_pos)
    return (outputs.reshape(-1, D), grad_in.reshape(-1, D), pooled, grads)

def reference(query_tokens, passage_tokens, query_cotangent, passage_cotangent, query_segments, passage_segments, query_cls, passage_cls, query_weight, query_bias, key_weight, value_weight, value_bias, out_weight, out_bias, norm1_gain, norm1_bias, inner_weight, inner_bias, outer_weight, outer_bias, norm2_gain, norm2_bias):
    weights = (query_weight, query_bias, key_weight, value_weight, value_bias, out_weight, out_bias, norm1_gain, norm1_bias, inner_weight, inner_bias, outer_weight, outer_bias, norm2_gain, norm2_bias)
    inputs_list = ((query_tokens, query_cotangent, query_segments, query_cls), (passage_tokens, passage_cotangent, passage_segments, passage_cls))
    towers = []
    for tower_index in range(2):
        params = tuple((member[tower_index].astype(jnp.float32) for member in weights))
        tokens, cotangent, labels, cls_pos = inputs_list[tower_index]
        towers.append(tower_reference(tokens, cotangent, labels, cls_pos, params))
    grads = [jnp.stack([towers[0][3][slot], towers[1][3][slot]]) for slot in range(15)]
    return (towers[0][0], towers[1][0], towers[0][1], towers[1][1], towers[0][2], towers[1][2], grads[0], grads[1], grads[2], grads[3], grads[4], grads[5], grads[6], grads[7], grads[8], grads[9], grads[10], grads[11], grads[12], grads[13], grads[14])
```

```python
import math

import jax
import jax.numpy as jnp
from jax import lax
from jax.sharding import PartitionSpec as P

HDIM = 64
NORM_EPS = 1e-05
MASKED = -1e30
D = 768
BLK = 128
QUERY_AT = 2
ROW_OF = (1, 2, 0, 3)


def matmul(left, right):
    return jnp.dot(left, right, preferred_element_type=jnp.float32)


def matmul_left(left, right):
    return lax.dot_general(
        left, right, (((0,), (0,)), ((), ())), preferred_element_type=jnp.float32
    )


def matmul_right(left, right):
    return lax.dot_general(
        left, right, (((1,), (1,)), ((), ())), preferred_element_type=jnp.float32
    )


def layer_norm(values, gain, bias):
    centred = values - jnp.mean(values, -1, keepdims=True)
    inverse = lax.rsqrt(jnp.mean(centred * centred, -1, keepdims=True) + NORM_EPS)
    normed = centred * inverse
    return (normed * gain + bias, normed, inverse)


def norm_back(upstream, normed, inverse, gain):
    scaled = upstream * gain
    return inverse * (
        scaled
        - jnp.mean(scaled, -1, keepdims=True)
        - normed * jnp.mean(scaled * normed, -1, keepdims=True)
    )


def gelu_slope(values):
    return 0.5 * (1.0 + lax.erf(values * (1.0 / math.sqrt(2.0)))) + values * jnp.exp(
        -0.5 * values * values
    ) * (1.0 / math.sqrt(2.0 * math.pi))


def attend(queries, key_vecs, value_vecs, allowed, scaling):
    scores = (
        jnp.einsum("qhd,khd->hqk", queries, key_vecs, preferred_element_type=jnp.float32) * scaling
    )
    row_top = jnp.max(jnp.where(allowed, scores, MASKED), -1, keepdims=True)
    unnorm = jnp.exp(jnp.where(allowed, scores - row_top, MASKED))
    totals = jnp.maximum(jnp.sum(unnorm, -1, keepdims=True), 1.0)
    probs = (unnorm / totals).astype(jnp.bfloat16)
    attended = jnp.einsum("hqk,khd->qhd", probs, value_vecs, preferred_element_type=jnp.float32)
    return (attended, row_top + jnp.log(totals))


def attend_back(queries, key_vecs, value_vecs, allowed, log_total, upstream, scaling):
    scores = (
        jnp.einsum("qhd,khd->hqk", queries, key_vecs, preferred_element_type=jnp.float32) * scaling
    )
    probs = jnp.exp(jnp.where(allowed, scores - log_total, MASKED))
    grad_value = jnp.einsum(
        "hqk,qhd->khd", probs.astype(jnp.bfloat16), upstream, preferred_element_type=jnp.float32
    )
    grad_probs = jnp.einsum(
        "qhd,khd->hqk", upstream, value_vecs, preferred_element_type=jnp.float32
    )
    grad_scores = (probs * (grad_probs - jnp.sum(probs * grad_probs, -1, keepdims=True))).astype(
        jnp.bfloat16
    )
    grad_query = (
        jnp.einsum("hqk,khd->qhd", grad_scores, key_vecs, preferred_element_type=jnp.float32)
        * scaling
    )
    grad_key = (
        jnp.einsum("hqk,qhd->khd", grad_scores, queries, preferred_element_type=jnp.float32)
        * scaling
    )
    return (grad_query, grad_key, grad_value)


def pick(stack, index):
    return lax.dynamic_index_in_dim(stack, index, 0, keepdims=False)


def build(wide):
    bits = [1 << i for i in range(1, wide.bit_length() - 1)]
    orders = (bits + [1], bits[::-1] + [1])

    def flip(values, bit):
        return lax.ppermute(values, "wide", [(i, i ^ bit) for i in range(wide)])

    def shift(values, step):
        return lax.ppermute(values, "narrow", [(i, (i + step) % 4) for i in range(4)])

    def route(values, pairs):
        return lax.ppermute(values, "narrow", pairs)

    def bit_of(index, bit):
        return (index // bit) % 2

    def piece_of(index, order):
        return sum(bit_of(index, bit) * (1 << i) for i, bit in enumerate(order))

    def gather(piece, order, me):
        for bit in order:
            other = flip(piece, bit)
            low = bit_of(me, bit) == 0
            piece = jnp.concatenate(
                [jnp.where(low, piece, other), jnp.where(low, other, piece)], -2
            )
        return piece

    def scatter(partial, order, me):
        for bit in order[::-1]:
            half = partial.shape[-2] // 2
            mine = bit_of(me, bit)
            sent = lax.dynamic_slice_in_dim(partial, (1 - mine) * half, half, -2)
            kept = lax.dynamic_slice_in_dim(partial, mine * half, half, -2)
            other = flip(sent.astype(jnp.bfloat16), bit)
            partial = kept.astype(jnp.float32) + other.astype(jnp.float32)
        return partial

    def to_rows(query, passage, at):
        local = jnp.concatenate([query, passage], 0).reshape(4, BLK, D)
        tables = jnp.array([[0, 1, 1, 0], [0, 0, 2, 0], [0, 0, 3, 0]], jnp.int32)[:, at]
        first = route(pick(local, tables[0]), [(1, 0), (2, 1), (0, 2)])
        second = route(pick(local, tables[1]), [(2, 1), (1, 2)])
        third = route(pick(local, tables[2]), [(2, 3), (3, 2)])
        every = jnp.concatenate([local, first[None], second[None], third[None]], 0)
        places = jnp.array(
            [[1, 2, 3, 4], [2, 3, 4, 5], [4, 5, 0, 6], [6, 1, 2, 3]], jnp.int32
        )[at]
        return jnp.concatenate([pick(every, places[j]) for j in range(4)], 0)

    def from_rows(row, at):
        local = row.reshape(4, BLK, D)
        tables = jnp.array([[3, 2, 0, 0], [0, 3, 1, 0], [0, 0, 3, 0]], jnp.int32)[:, at]
        first = route(pick(local, tables[0]), [(0, 1), (1, 2), (2, 0)])
        second = route(pick(local, tables[1]), [(1, 2), (2, 1)])
        third = route(pick(local, tables[2]), [(3, 2), (2, 3)])
        every = jnp.concatenate([local, first[None], second[None], third[None]], 0)
        places = jnp.array(
            [[4, 0, 1, 2], [5, 4, 0, 1], [2, 4, 5, 6], [6, 1, 2, 3]], jnp.int32
        )[at]
        query = pick(every, places[0])
        passage = jnp.concatenate([pick(every, places[j]) for j in range(1, 4)], 0)
        return query, passage

    def per_device(
        query_tokens,
        passage_tokens,
        query_cotangent,
        passage_cotangent,
        query_segments,
        passage_segments,
        query_cls,
        passage_cls,
        query_weight,
        query_bias,
        key_weight,
        value_weight,
        value_bias,
        out_weight,
        out_bias,
        norm1_gain,
        norm1_bias,
        inner_weight,
        inner_bias,
        outer_weight,
        outer_bias,
        norm2_gain,
        norm2_bias,
    ):
        at = lax.axis_index("narrow")
        me = lax.axis_index("wide")
        tower_at = jnp.array([1, 1, 0, 1], jnp.int32)
        own_tower = tower_at[at]
        row_at = jnp.array(ROW_OF, jnp.int32)[at]
        scaling = HDIM ** (-0.5)

        tokens = to_rows(query_tokens, passage_tokens, at)
        labels = pick(jnp.concatenate([query_segments, passage_segments], 0), row_at)
        cls_pos = pick(
            jnp.concatenate([query_cls, jnp.pad(passage_cls, ((0, 0), (0, 12)))], 0), row_at
        )

        turn = lambda w: jnp.swapaxes(w, 1, 2)
        streams = (
            jnp.concatenate([turn(query_weight), turn(key_weight)], 1),
            jnp.concatenate([turn(value_weight), out_weight], 1),
            inner_weight[:, :384],
            inner_weight[:, 384:],
            outer_weight[:, :384],
            outer_weight[:, 384:],
        )
        count = 384 // wide
        own, others = [], []
        for group in range(3):
            pair = streams[2 * group : 2 * group + 2]
            arrived = []
            for step in (1, 2, 3):
                goal = tower_at[(at + step) % 4]
                sent = [
                    lax.dynamic_slice(
                        stream, (goal, piece_of(me, orders[i]) * count, 0), (1, count, D)
                    )
                    for i, stream in enumerate(pair)
                ]
                arrived.append(shift(jnp.concatenate(sent, 0), step))
            arrived = jnp.stack(arrived, 1)
            for i in range(2):
                others.append(gather(arrived[i], orders[i], me))
                own.append(pick(pair[i], own_tower))

        small = jnp.concatenate([query_bias, value_bias, inner_bias], 1)
        small_rel = [pick(small, own_tower)]
        for step in (1, 2, 3):
            goal = tower_at[(at + step) % 4]
            small_rel.append(shift(pick(small, goal).reshape(9, 128), step).reshape(-1))
        small_rel = jnp.stack(small_rel, 0)
        bias_q = small_rel[:, :192].reshape(-1)
        bias_v = small_rel[:, 192:384].reshape(-1)
        bias_inner = small_rel[:, 384:]
        vec = lambda v: pick(v, own_tower)

        def joined(stream, low, high):
            return jnp.concatenate([own[stream][None, low:high], others[stream][:, low:high]], 0)

        w_q = joined(0, 0, 192).reshape(D, D)
        w_k = joined(0, 192, 384).reshape(D, D)
        w_v = joined(1, 0, 192).reshape(D, D)
        w_o = joined(1, 192, 384).reshape(D, D)
        part = lambda stream, k: own[stream] if k == 0 else others[stream][k - 1]
        w_in = [jnp.concatenate([part(2, k), part(3, k)], 0) for k in range(4)]
        w_out = [jnp.concatenate([part(4, k), part(5, k)], 0) for k in range(4)]

        split = (512, 12, HDIM)
        queries = (matmul_right(tokens, w_q) + bias_q).astype(jnp.bfloat16).reshape(split)
        key_vecs = matmul_right(tokens, w_k).astype(jnp.bfloat16).reshape(split)
        value_vecs = (matmul_right(tokens, w_v) + bias_v).astype(jnp.bfloat16).reshape(split)
        allowed = ((labels[:, None] == labels[None, :]) & (labels[None, :] >= 0))[None]
        attended, log_total = attend(queries, key_vecs, value_vecs, allowed, scaling)
        attended = attended.reshape(-1, D).astype(jnp.bfloat16)
        gain1, gain2 = vec(norm1_gain), vec(norm2_gain)
        hidden1, normed1, inverse1 = layer_norm(
            tokens.astype(jnp.float32) + matmul(attended, w_o) + vec(out_bias),
            gain1,
            vec(norm1_bias),
        )
        hidden = hidden1.astype(jnp.bfloat16)
        inner_pre = [matmul(hidden, w_in[k]) + bias_inner[k] for k in range(4)]
        activated = [
            jax.nn.gelu(inner_pre[k], approximate=False).astype(jnp.bfloat16) for k in range(4)
        ]
        ffn_out = sum(matmul(activated[k], w_out[k]) for k in range(4))
        result, normed2, inverse2 = layer_norm(
            hidden1 + ffn_out + vec(outer_bias), gain2, vec(norm2_bias)
        )
        result = result.astype(jnp.bfloat16)
        query_out, passage_out = from_rows(result, at)

        picked = (cls_pos[:, None] == jnp.arange(512, dtype=jnp.int32)[None, :]).astype(
            jnp.bfloat16
        )
        heads_of = matmul(picked, result).astype(jnp.bfloat16)
        pooled = jnp.stack([heads_of] + [shift(heads_of, step) for step in (1, 2, 3)], 0)
        pooled = pick(jnp.moveaxis(pooled.reshape(4, 16, 4, 192), 2, 0), at)
        query_pooled = pick(pooled, (at - QUERY_AT) % 4)[None]
        passage_pooled = jnp.stack(
            [pick(pooled, (at - source) % 4)[:4] for source in (0, 1, 3)], 0
        )

        cot_rows = to_rows(query_cotangent, passage_cotangent, at).astype(jnp.float32)
        grad_gain2 = jnp.sum(cot_rows * normed2, 0)
        grad_bias2 = jnp.sum(cot_rows, 0)
        grad_resid2 = norm_back(cot_rows, normed2, inverse2, gain2)
        grad_outer_bias = jnp.sum(grad_resid2, 0)
        d2 = grad_resid2.astype(jnp.bfloat16)
        low = jnp.bfloat16
        grad_outer = jnp.stack([matmul_left(activated[k], d2).astype(low) for k in range(4)], 0)
        grad_inner_pre = [
            (matmul_right(d2, w_out[k]) * gelu_slope(inner_pre[k])).astype(jnp.bfloat16)
            for k in range(4)
        ]
        grad_inner = jnp.stack(
            [matmul_left(hidden, grad_inner_pre[k]).astype(low) for k in range(4)], 0
        )
        grad_inner_bias = [
            jnp.sum(grad_inner_pre[k], 0, dtype=jnp.float32) for k in range(4)
        ]
        grad_hidden1 = (
            sum(matmul_right(grad_inner_pre[k], w_in[k]) for k in range(4)) + grad_resid2
        )
        grad_gain1 = jnp.sum(grad_hidden1 * normed1, 0)
        grad_bias1 = jnp.sum(grad_hidden1, 0)
        grad_resid1 = norm_back(grad_hidden1, normed1, inverse1, gain1)
        grad_out_bias = jnp.sum(grad_resid1, 0)
        d1 = grad_resid1.astype(jnp.bfloat16)
        grad_out = matmul_left(attended, d1).astype(low)
        grad_attended = matmul_right(d1, w_o).astype(jnp.bfloat16).reshape(split)
        grad_query, grad_key, grad_value = attend_back(
            queries, key_vecs, value_vecs, allowed, log_total, grad_attended, scaling
        )
        grad_query = grad_query.reshape(-1, D).astype(jnp.bfloat16)
        grad_key = grad_key.reshape(-1, D).astype(jnp.bfloat16)
        grad_value = grad_value.reshape(-1, D).astype(jnp.bfloat16)
        by_shard = lambda g: g.astype(low).reshape(4, 192, D)
        grad_streams = (
            jnp.concatenate(
                [by_shard(matmul_left(grad_query, tokens)), by_shard(matmul_left(grad_key, tokens))],
                1,
            ),
            jnp.concatenate([by_shard(matmul_left(grad_value, tokens)), by_shard(grad_out)], 1),
            grad_inner[:, :384],
            grad_inner[:, 384:],
            grad_outer[:, :384],
            grad_outer[:, 384:],
        )
        grad_in = (
            matmul(grad_query, w_q) + matmul(grad_key, w_k) + matmul(grad_value, w_v) + grad_resid1
        ).astype(jnp.bfloat16)
        query_grad_in, passage_grad_in = from_rows(grad_in, at)

        full = [None] * 6
        for group in (2, 1, 0):
            summed = [
                scatter(grad_streams[2 * group + i], orders[i], me).astype(jnp.bfloat16)
                for i in range(2)
            ]
            block = jnp.stack(summed, 1)
            parts = [block[0]] + [shift(block[k], -k) for k in (1, 2, 3)]
            towers = []
            for tower in range(2):
                towers.append(
                    sum(
                        jnp.where(
                            tower_at[(at + k) % 4] == tower, parts[k].astype(jnp.float32), 0.0
                        )
                        for k in range(4)
                    ).astype(jnp.bfloat16)
                )
            both = jnp.stack(towers, 1)
            for i in range(2):
                full[2 * group + i] = gather(both[i], orders[i], me)

        absolute = lambda rel: jnp.stack([pick(rel, (at - s) % 4) for s in range(4)], 0)
        vectors = jnp.concatenate(
            [
                absolute(jnp.sum(grad_query, 0, dtype=jnp.float32).reshape(4, 192)).reshape(1, D),
                absolute(jnp.sum(grad_value, 0, dtype=jnp.float32).reshape(4, 192)).reshape(1, D),
                absolute(jnp.stack(grad_inner_bias, 0)),
                jnp.stack(
                    [
                        grad_out_bias,
                        grad_gain1,
                        grad_bias1,
                        grad_outer_bias,
                        grad_gain2,
                        grad_bias2,
                    ],
                    0,
                ),
            ],
            0,
        )
        for bit in orders[0]:
            vectors = vectors + flip(vectors, bit)
        spread = [vectors] + [shift(vectors, step) for step in (1, 2, 3)]
        vectors = jnp.stack(
            [
                sum(
                    jnp.where(tower_at[(at - step) % 4] == tower, spread[step], 0.0)
                    for step in range(4)
                )
                for tower in range(2)
            ],
            0,
        )
        here = lambda row: pick(jnp.swapaxes(vectors[:, row].reshape(2, 4, 192), 0, 1), at)
        wide_f = lambda g: g.astype(jnp.float32)
        return (
            query_out,
            passage_out,
            query_grad_in,
            passage_grad_in,
            query_pooled,
            passage_pooled,
            wide_f(turn(full[0][:, :192])),
            here(0),
            wide_f(turn(full[0][:, 192:])),
            wide_f(turn(full[1][:, :192])),
            here(1),
            wide_f(full[1][:, 192:]),
            vectors[:, 6],
            vectors[:, 7],
            vectors[:, 8],
            wide_f(jnp.concatenate([full[2], full[3]], 1)),
            pick(jnp.swapaxes(vectors[:, 2:6], 0, 1), at),
            wide_f(jnp.concatenate([full[4], full[5]], 1)),
            vectors[:, 9],
            vectors[:, 10],
            vectors[:, 11],
        )

    return per_device


def solution(mesh):
    rows = P(("wide", "narrow"), None)
    by_wide = P("wide", None)
    cols = P(None, None, "narrow")
    mids = P(None, "narrow", None)
    flat = P(None, "narrow")
    return jax.shard_map(
        build(mesh.shape["wide"]),
        mesh=mesh,
        in_specs=(rows,) * 4
        + (by_wide,) * 4
        + (cols, flat, cols, cols, flat, mids, P(), P(), P(), cols, flat, mids, P(), P(), P()),
        out_specs=(rows,) * 4
        + (P("wide", None, "narrow"),) * 2
        + (cols, flat, cols, cols, flat, mids, P(), P(), P(), cols, flat, mids, P(), P(), P()),
        check_vma=False,
    )
```

```python
import math

import jax
import jax.numpy as jnp
import numpy as np
from jax import lax
from jax.experimental import pallas as pl
from jax.experimental.pallas import tpu as pltpu
from jax.sharding import PartitionSpec as P

NORM_EPS = 1e-05
HIDE = -1e30
FLOOR = -1e29
TILE = 512
D = 768
BLK = 128
QUERY_AT = 2
ROW_OF = (1, 2, 0, 3)


def matmul(left, right):
    return jnp.dot(left, right, preferred_element_type=jnp.float32)


def matmul_left(left, right):
    return lax.dot_general(
        left, right, (((0,), (0,)), ((), ())), preferred_element_type=jnp.float32
    )


def matmul_right(left, right):
    return lax.dot_general(
        left, right, (((1,), (1,)), ((), ())), preferred_element_type=jnp.float32
    )


def layer_norm(values, gain, bias):
    centred = values - jnp.mean(values, -1, keepdims=True)
    inverse = lax.rsqrt(jnp.mean(centred * centred, -1, keepdims=True) + NORM_EPS)
    normed = centred * inverse
    return (normed * gain + bias, normed, inverse)


def norm_back(upstream, normed, inverse, gain):
    scaled = upstream * gain
    return inverse * (
        scaled
        - jnp.mean(scaled, -1, keepdims=True)
        - normed * jnp.mean(scaled * normed, -1, keepdims=True)
    )


def gelu_slope(values):
    return 0.5 * (1.0 + lax.erf(values * (1.0 / math.sqrt(2.0)))) + values * jnp.exp(
        -0.5 * values * values
    ) * (1.0 / math.sqrt(2.0 * math.pi))


def cross(left, right):
    return lax.dot_general(
        left, right, (((1,), (1,)), ((), ())), preferred_element_type=jnp.float32
    )


def inward(left, right):
    return lax.dot_general(
        left, right, (((0,), (0,)), ((), ())), preferred_element_type=jnp.float32
    )


def attend_kernel(q_ref, k_ref, v_ref, row_ref, col_ref, out_ref, lse_ref, bias_ref):
    length = q_ref.shape[0]

    @pl.when(pl.program_id(0) == 0)
    def _():
        keys = col_ref[...]
        bias_ref[...] = jnp.where((row_ref[...] == keys) & (keys >= 0), 0.0, HIDE)

    key_vecs, value_vecs = k_ref[...], v_ref[...]
    low = lax.broadcasted_iota(jnp.int32, (length, 128), 1) < 64
    zero = jnp.bfloat16(0)
    key_half = [jnp.where(low == (head == 0), key_vecs, zero) for head in range(2)]
    for start in range(0, length, TILE):
        rows = pl.ds(start, TILE)
        queries = q_ref[rows, :] * jnp.bfloat16(0.125)
        outs = []
        for head in range(2):
            scores = cross(key_half[head], queries) + bias_ref[:, rows]
            top = jnp.maximum(jnp.max(scores, 0, keepdims=True), FLOOR)
            unnorm = jnp.exp(scores - top)
            total = jnp.maximum(jnp.sum(unnorm, 0, keepdims=True), 1.0)
            probs = (unnorm * (1.0 / total)).astype(jnp.bfloat16)
            outs.append(inward(probs, value_vecs))
            lse_ref[0, head : head + 1, rows] = top + jnp.log(total)
        out_ref[rows, :] = jnp.where(low[:TILE], outs[0], outs[1]).astype(jnp.bfloat16)


def attend_back_kernel(
    q_ref, k_ref, v_ref, up_ref, lse_ref, row_ref, col_ref, dq_ref, dk_ref, dv_ref, bias_ref
):
    length = q_ref.shape[0]

    @pl.when(pl.program_id(0) == 0)
    def _():
        keys = col_ref[...]
        bias_ref[...] = jnp.where((row_ref[...] == keys) & (keys >= 0), 0.0, HIDE)

    key_vecs, value_vecs = k_ref[...], v_ref[...]
    low = lax.broadcasted_iota(jnp.int32, (length, 128), 1) < 64
    low_tile = low[:TILE]
    dk = [jnp.zeros((length, 128), jnp.float32)] * 2
    dv = [jnp.zeros((length, 128), jnp.float32)] * 2
    zero = jnp.bfloat16(0)
    key_half = [jnp.where(low == (head == 0), key_vecs, zero) for head in range(2)]
    value_half = [jnp.where(low == (head == 0), value_vecs, zero) for head in range(2)]
    for start in range(0, length, TILE):
        rows = pl.ds(start, TILE)
        queries = q_ref[rows, :] * jnp.bfloat16(0.125)
        upstream = up_ref[rows, :]
        dq = []
        for head in range(2):
            scores = cross(key_half[head], queries) + bias_ref[:, rows]
            probs = jnp.exp(scores - lse_ref[0, head : head + 1, rows])
            grad_probs = cross(value_half[head], upstream)
            mean = jnp.sum(probs * grad_probs, 0, keepdims=True)
            grad_scores = (probs * (grad_probs - mean)).astype(jnp.bfloat16)
            dv[head] = dv[head] + jnp.dot(
                probs.astype(jnp.bfloat16), upstream, preferred_element_type=jnp.float32
            )
            dk[head] = dk[head] + jnp.dot(
                grad_scores, queries, preferred_element_type=jnp.float32
            )
            dq.append(inward(grad_scores, key_vecs))
        dq_ref[rows, :] = (jnp.where(low_tile, dq[0], dq[1]) * 0.125).astype(jnp.bfloat16)
    dk_ref[...] = jnp.where(low, dk[0], dk[1]).astype(jnp.bfloat16)
    dv_ref[...] = jnp.where(low, dv[0], dv[1]).astype(jnp.bfloat16)


def attend(queries, key_vecs, value_vecs, labels):
    length, width = queries.shape
    pairs = width // 128
    lane = pl.BlockSpec((length, 128), lambda i: (0, i))
    return pl.pallas_call(
        attend_kernel,
        grid=(pairs,),
        in_specs=[
            lane,
            lane,
            lane,
            pl.BlockSpec((1, length), lambda i: (0, 0)),
            pl.BlockSpec((length, 1), lambda i: (0, 0)),
        ],
        out_specs=[lane, pl.BlockSpec((1, 2, length), lambda i: (i, 0, 0))],
        out_shape=[
            jax.ShapeDtypeStruct((length, width), jnp.bfloat16),
            jax.ShapeDtypeStruct((pairs, 2, length), jnp.float32),
        ],
        scratch_shapes=[pltpu.VMEM((length, length), jnp.float32)],
        cost_estimate=pl.CostEstimate(
            flops=4 * length * length * width,
            bytes_accessed=8 * length * width,
            transcendentals=length * length * width // 64,
        ),
        compiler_params=pltpu.CompilerParams(vmem_limit_bytes=24 << 20),
        name="attend",
    )(queries, key_vecs, value_vecs, labels[None, :], labels[:, None])


def attend_back(queries, key_vecs, value_vecs, upstream, log_total, labels):
    length, width = queries.shape
    pairs = width // 128
    lane = pl.BlockSpec((length, 128), lambda i: (0, i))
    return pl.pallas_call(
        attend_back_kernel,
        grid=(pairs,),
        in_specs=[
            lane,
            lane,
            lane,
            lane,
            pl.BlockSpec((1, 2, length), lambda i: (i, 0, 0)),
            pl.BlockSpec((1, length), lambda i: (0, 0)),
            pl.BlockSpec((length, 1), lambda i: (0, 0)),
        ],
        out_specs=[lane, lane, lane],
        out_shape=[jax.ShapeDtypeStruct((length, width), jnp.bfloat16)] * 3,
        scratch_shapes=[pltpu.VMEM((length, length), jnp.float32)],
        cost_estimate=pl.CostEstimate(
            flops=10 * length * length * width,
            bytes_accessed=16 * length * width,
            transcendentals=length * length * width // 64,
        ),
        compiler_params=pltpu.CompilerParams(vmem_limit_bytes=32 << 20),
        name="attend_back",
    )(queries, key_vecs, value_vecs, upstream, log_total, labels[None, :], labels[:, None])


def tie(value, *after):
    return lax.optimization_barrier((value, after))[0]


def cases(at, *bodies):
    for n, body in enumerate(bodies):
        pl.when(at == n)(body)


def build(wide):
    bits = [1 << i for i in range(1, wide.bit_length() - 1)]
    orders = (bits + [1], bits[::-1] + [1])
    last = len(bits)
    half = wide // 2
    count = 384 // wide
    tile = (count, D)

    def mover(name, kernel, ins, outs, scratch=(), limit=16 << 20):
        pairs = [item if isinstance(item, tuple) else (item, pltpu.VMEM) for item in ins]
        return pl.pallas_call(
            kernel,
            in_specs=[pl.BlockSpec(memory_space=space) for _, space in pairs],
            out_specs=[pl.BlockSpec(memory_space=pltpu.VMEM)] * len(outs),
            out_shape=[jax.ShapeDtypeStruct(shape, dtype) for shape, dtype in outs],
            scratch_shapes=list(scratch),
            compiler_params=pltpu.CompilerParams(vmem_limit_bytes=limit),
            name=name,
        )(*[array for array, _ in pairs])

    low = jnp.bfloat16

    def narrow_at():
        return lax.axis_index("narrow")

    def bit_at(bit):
        return lax.rem(lax.div(lax.axis_index("wide"), bit), 2)

    def piece_at(order):
        return sum(bit_at(bit) * (1 << j) for j, bit in enumerate(order))

    def tower_of(n):
        return jnp.where(n == QUERY_AT, 0, 1)

    def flip(values, bit):
        return lax.ppermute(values, "wide", [(i, i ^ bit) for i in range(wide)])

    def route(values, pairs):
        return lax.ppermute(values, "narrow", pairs)

    def shift(values, step):
        return route(values, [(i, (i + step) % 4) for i in range(4)])

    def swap(values):
        return lax.all_to_all(values, "narrow", 0, 0, tiled=True)

    def pack(*groups):
        flat = [member for group in groups for member in group]

        def kernel(*refs):
            sources, outs, sem = refs[: len(flat)], refs[len(flat) : -1], refs[-1]
            copies = []
            for g in range(len(groups)):
                for step in (1, 2, 3):
                    tower = tower_of(lax.rem(narrow_at() + step, 4))
                    for i in range(2):
                        base = flat[2 * g + i][1]
                        copies.append(
                            pltpu.make_async_copy(
                                sources[2 * g + i].at[tower, base + piece_at(orders[i])],
                                outs[3 * g + step - 1].at[i],
                                sem.at[len(copies)],
                            )
                        )
            for copy in copies:
                copy.start()
            for copy in copies:
                copy.wait()

        count_out = 3 * len(groups)
        out = mover(
            "pack",
            kernel,
            [(array, pl.ANY) for array, _ in flat],
            [((2,) + tile, low)] * count_out,
            [pltpu.SemaphoreType.DMA((2 * count_out,))],
        )
        return [out[3 * g : 3 * g + 3] for g in range(len(groups))]

    def sent(messages, scope):
        with jax.named_scope(scope):
            return [shift(message, step + 1) for step, message in enumerate(messages)]

    def unpack(arrived):
        def kernel(*refs):
            for k in range(3):
                for i in range(2):
                    refs[3 + i][k, 0] = refs[k][i]

        return mover("unpack", kernel, arrived, [((3, 1) + tile, low)] * 2)

    def doubled(pair, others, step):
        slots, have = pair[0].shape[:2]
        merged = step == last - 1

        def kernel(a_ref, ra_ref, b_ref, rb_ref, *out_refs):
            for i, (mine, other) in enumerate(((a_ref, ra_ref), (b_ref, rb_ref))):
                bit = bit_at(orders[i][step])
                out = out_refs[0].at[i] if merged else out_refs[i]
                for k in range(slots):
                    out[k, pl.ds(bit * have, have)] = mine[k]
                    out[k, pl.ds((1 - bit) * have, have)] = other[k]

        shape = (slots, 2 * have) + tile
        outs = [((2,) + shape, low)] if merged else [(shape, low)] * 2
        return mover("doubled", kernel, [pair[0], others[0], pair[1], others[1]], outs)

    def spread(pair, scope):
        for step in range(last):
            with jax.named_scope(f"{scope}{step}"):
                others = [flip(pair[i], orders[i][step]) for i in range(2)]
            pair = doubled(pair, others, step)
        return pair[0]

    def finish(mine, other, group, by_kind):
        def kernel(a_ref, b_ref, mine_ref, other_ref, out_ref, sem):
            tower = tower_of(narrow_at())
            bit = bit_at(1)
            copies = []
            for i, source in enumerate((a_ref, b_ref)):
                for h in range(2):
                    place = (i, h, 0) if by_kind else (0, i, h)
                    copies.append(
                        pltpu.make_async_copy(
                            source.at[tower, pl.ds(group[i][1] + h * half, half)],
                            out_ref.at[place],
                            sem.at[2 * i + h],
                        )
                    )
            for copy in copies:
                copy.start()
            for k in range(3):
                for i in range(2):
                    for h, source in ((bit, mine_ref), (1 - bit, other_ref)):
                        place = (i, h, k + 1) if by_kind else (k + 1, i, h)
                        out_ref[place] = source[i, k]
            for copy in copies:
                copy.wait()

        shape = (2, 2, 4, half) if by_kind else (4, 2, 2, half)
        return mover(
            "finish",
            kernel,
            [(group[0][0], pl.ANY), (group[1][0], pl.ANY), mine, other],
            [(shape + tile, low)],
            [pltpu.SemaphoreType.DMA((4,))],
            limit=24 << 20,
        )[0]

    def split_kinds(kinds):
        def kernel(q_ref, k_ref, v_ref, o_ref, sent_ref, kept_ref):
            bit = bit_at(1)
            for n, (to_high, to_low) in enumerate(((sent_ref, kept_ref), (kept_ref, sent_ref))):

                @pl.when(bit == n)
                def _():
                    for i, (lower, upper) in enumerate(((q_ref, k_ref), (v_ref, o_ref))):
                        to_high[i] = upper[...]
                        to_low[i] = lower[...]

        shape = (2, 4, half) + tile
        return mover(
            "split",
            kernel,
            [g.reshape((4, half) + tile) for g in kinds],
            [(shape, low)] * 2,
            limit=24 << 20,
        )

    def split_slots(slots):
        def kernel(*refs):
            bit = bit_at(1)
            sent_ref, kept_ref = refs[4:]
            for i in range(2):
                for k in range(4):
                    sent_ref[i, k] = refs[k][i, 1 - bit]
                    kept_ref[i, k] = refs[k][i, bit]

        shape = (2, 4, half) + tile
        return mover(
            "split",
            kernel,
            [g.reshape((2, 2, half) + tile) for g in slots],
            [(shape, low)] * 2,
            limit=24 << 20,
        )

    def added(left, right):
        return (left.astype(jnp.float32) + right.astype(jnp.float32)).astype(low)

    def halved(kept, others, step):
        merged = step == last
        have = half if merged else kept[0].shape[1]

        def kernel(*refs):
            for i in range(2):
                sent_ref, kept_ref = refs[-4 + 2 * i], refs[-3 + 2 * i]
                bit = bit_at(orders[i][step - 1])
                for h, out_ref in ((1 - bit, sent_ref), (bit, kept_ref)):
                    part = pl.ds(h * (have // 2), have // 2)
                    for k in range(4):
                        if merged:
                            out_ref[k] = added(refs[0][i, k, part], refs[1][i, k, part])
                        else:
                            out_ref[k] = added(refs[2 * i][k, part], refs[2 * i + 1][k, part])

        ins = [kept, others] if merged else [kept[0], others[0], kept[1], others[1]]
        return mover("halved", kernel, ins, [((4, have // 2) + tile, low)] * 4)

    def address(kept, others):
        def kernel(a_ref, ra_ref, b_ref, rb_ref, *out_refs):
            for k in range(4):
                out_refs[k][0] = added(a_ref[k, 0], ra_ref[k, 0])
                out_refs[k][1] = added(b_ref[k, 0], rb_ref[k, 0])

        ins = [kept[0], others[0], kept[1], others[1]]
        return mover("address", kernel, ins, [((2,) + tile, low)] * 4)

    def by_tower(arrived):
        def kernel(*refs):
            weights = [
                jnp.where(lax.rem(narrow_at() + k, 4) == QUERY_AT, 1.0, 0.0) for k in range(4)
            ]
            for i in range(2):
                values = [refs[k][i].astype(jnp.float32) for k in range(4)]
                query = sum(w * v for w, v in zip(weights, values))
                passage = sum((1.0 - w) * v for w, v in zip(weights, values))
                refs[4 + i][0, 0] = query.astype(low)
                refs[4 + i][1, 0] = passage.astype(low)

        return mover("by_tower", kernel, arrived, [((2, 1) + tile, low)] * 2)

    def widen(mine, other, by_kind):
        def kernel(mine_ref, other_ref, out_ref):
            bit = bit_at(1)
            for t in range(2):
                for i in range(2):
                    for h, source in ((bit, mine_ref), (1 - bit, other_ref)):
                        place = (i, h, t) if by_kind else (t, i, h)
                        out_ref[place] = source[i, t].astype(jnp.float32)

        out = ((2, 2, 2, half) + tile, jnp.float32)
        return mover("widen", kernel, [mine, other], [out], limit=24 << 20)[0]

    def to_rows(query, passage, scope):
        block = (BLK, D)
        passage = passage.reshape((3,) + block)

        def first_kernel(q_ref, p_ref, a_ref, b_ref, c_ref):
            at = narrow_at()
            a_ref[...] = jnp.where(at == 0, q_ref[...], p_ref[0])
            b_ref[...] = jnp.where(at == 2, p_ref[1], q_ref[...])
            c_ref[...] = jnp.where(at == 2, p_ref[2], q_ref[...])

        parts = mover("row_parts", first_kernel, [query, passage], [(block, low)] * 3)
        with jax.named_scope(scope):
            a = route(parts[0], [(1, 0), (2, 1), (0, 2)])
            b = route(parts[1], [(2, 1), (1, 2)])
            c = route(parts[2], [(2, 3), (3, 2)])

        def last_kernel(q_ref, p_ref, a_ref, b_ref, c_ref, out_ref):
            def fill(*parts):
                def body():
                    for j, part in enumerate(parts):
                        out_ref[j] = part()

                return body

            p = [lambda j=j: p_ref[j] for j in range(3)]
            q, a, b, c = (lambda r=r: r[...] for r in (q_ref, a_ref, b_ref, c_ref))
            cases(
                narrow_at(),
                fill(p[0], p[1], p[2], a),
                fill(p[1], p[2], a, b),
                fill(a, b, q, c),
                fill(c, p[0], p[1], p[2]),
            )

        return mover("row_joined", last_kernel, [query, passage, a, b, c], [((4,) + block, low)])[
            0
        ].reshape(4 * BLK, D)

    def from_rows(row, scope):
        block = (BLK, D)
        row = row.reshape((4,) + block)

        def first_kernel(r_ref, a_ref, b_ref, c_ref):
            at = narrow_at()
            a_ref[...] = r_ref[jnp.where(at == 0, 3, jnp.where(at == 1, 2, 0))]
            b_ref[...] = r_ref[jnp.where(at == 1, 3, 1)]
            c_ref[...] = r_ref[jnp.where(at == 2, 3, 0)]

        parts = mover("own_parts", first_kernel, [row], [(block, low)] * 3)
        with jax.named_scope(scope):
            a = route(parts[0], [(0, 1), (1, 2), (2, 0)])
            b = route(parts[1], [(1, 2), (2, 1)])
            c = route(parts[2], [(3, 2), (2, 3)])

        def last_kernel(r_ref, a_ref, b_ref, c_ref, q_ref, p_ref):
            def fill(*parts):
                def body():
                    q_ref[...] = parts[0]()
                    for j in range(3):
                        p_ref[j] = parts[1 + j]()

                return body

            r = [lambda j=j: r_ref[j] for j in range(4)]
            a, b, c = (lambda ref=ref: ref[...] for ref in (a_ref, b_ref, c_ref))
            cases(
                narrow_at(),
                fill(a, r[0], r[1], r[2]),
                fill(b, a, r[0], r[1]),
                fill(r[2], a, b, c),
                fill(c, r[1], r[2], r[3]),
            )

        query, passage = mover(
            "own_joined", last_kernel, [row, a, b, c], [(block, low), ((3,) + block, low)]
        )
        return query, passage.reshape(3 * BLK, D)

    def per_device(
        query_tokens,
        passage_tokens,
        query_cotangent,
        passage_cotangent,
        query_segments,
        passage_segments,
        query_cls,
        passage_cls,
        query_weight,
        query_bias,
        key_weight,
        value_weight,
        value_bias,
        out_weight,
        out_bias,
        norm1_gain,
        norm1_bias,
        inner_weight,
        inner_bias,
        outer_weight,
        outer_bias,
        norm2_gain,
        norm2_bias,
    ):
        at = lax.axis_index("narrow").astype(jnp.uint32)

        def pick(stack, index):
            zeros = (jnp.uint32(0),) * (stack.ndim - 1)
            sizes = (1,) + stack.shape[1:]
            return lax.dynamic_slice(stack, (index,) + zeros, sizes).reshape(sizes[1:])

        def turned(slots):
            back = jnp.flip(slots, 0)
            zeros = (jnp.uint32(0),) * (slots.ndim - 1)
            return lax.dynamic_slice(
                jnp.concatenate([back, back], 0), (jnp.uint32(3) - at,) + zeros, slots.shape
            )

        query_role = at == QUERY_AT
        turn = lambda w: jnp.swapaxes(w, 1, 2)
        pieces = lambda w: w.reshape((2, -1) + tile)
        qk = pieces(jnp.concatenate([turn(query_weight), turn(key_weight)], 1))
        vo = pieces(jnp.concatenate([turn(value_weight), out_weight], 1))
        inner_all, outer_all = pieces(inner_weight), pieces(outer_weight)
        groups = (
            ((qk, 0), (vo, 0)),
            ((inner_all, 0), (inner_all, wide)),
            ((outer_all, 0), (outer_all, wide)),
        )

        arrived0 = sent(pack(groups[0])[0], "z0")
        tokens = to_rows(query_tokens, passage_tokens, "rows_x")
        small = jnp.concatenate([query_bias, value_bias, inner_bias], 1)
        with jax.named_scope("biases"):
            small = swap(jnp.stack([small[0 if n == QUERY_AT else 1] for n in range(4)], 0))
        packed = pack(groups[1], groups[2])
        arrived1 = sent([tie(m, *arrived0) for m in packed[0]], "z1")
        arrived2 = sent([tie(m, *arrived1) for m in packed[1]], "z2")

        def group_weights(group, arrived):
            mine = spread(unpack(arrived), f"ag{group}_")
            with jax.named_scope(f"ag{group}_core"):
                other = flip(mine, 1)
            return finish(mine, other, groups[group], group == 0)

        labels = jnp.where(
            query_role, query_segments[0], pick(passage_segments, jnp.minimum(at, 2))
        )
        cls_pos = jnp.where(
            query_role,
            query_cls[0],
            pick(jnp.pad(passage_cls, ((0, 0), (0, 12))), jnp.minimum(at, 2)),
        )
        small = turned(small)
        bias_q = small[:, :192].reshape(-1)
        bias_v = small[:, 192:384].reshape(-1)
        bias_inner = small[:, 384:]
        vecs = jnp.stack([out_bias, norm1_gain, norm1_bias, outer_bias, norm2_gain, norm2_bias], 1)
        vecs = jnp.where(query_role, vecs[0], vecs[1])

        attn_w = group_weights(0, arrived0).reshape(4, D, D)
        w_q, w_k, w_v, w_o = (attn_w[i] for i in range(4))

        queries = (matmul_right(tokens, w_q) + bias_q).astype(low)
        key_vecs = matmul_right(tokens, w_k).astype(low)
        value_vecs = (matmul_right(tokens, w_v) + bias_v).astype(low)
        attended, log_total = attend(queries, key_vecs, value_vecs, labels)
        cot_rows = to_rows(
            tie(query_cotangent, *arrived2), tie(passage_cotangent, *arrived2), "rows_c"
        )
        gain1, gain2 = vecs[1], vecs[4]
        hidden1, normed1, inverse1 = layer_norm(
            tokens.astype(jnp.float32) + matmul(attended, w_o) + vecs[0], gain1, vecs[2]
        )
        hidden = hidden1.astype(low)
        w_in = group_weights(1, arrived1).reshape(4, D, D)
        inner_pre = [matmul(hidden, w_in[k]) + bias_inner[k] for k in range(4)]
        activated = [jax.nn.gelu(inner_pre[k], approximate=False).astype(low) for k in range(4)]
        w_out = group_weights(2, arrived2).reshape(4, D, D)
        ffn_out = sum(matmul(activated[k], w_out[k]) for k in range(4))
        result, normed2, inverse2 = layer_norm(hidden1 + ffn_out + vecs[3], gain2, vecs[5])
        result = result.astype(low)

        cot_rows = cot_rows.astype(jnp.float32)
        grad_gain2 = jnp.sum(cot_rows * normed2, 0)
        grad_bias2 = jnp.sum(cot_rows, 0)
        grad_resid2 = norm_back(cot_rows, normed2, inverse2, gain2)
        grad_outer_bias = jnp.sum(grad_resid2, 0)
        d2 = grad_resid2.astype(low)

        def cores(parts, scope):
            sent, kept = parts
            with jax.named_scope(scope + "core"):
                return kept, flip(sent, 1)

        def reduced(kept, other, scope):
            step = last
            while step > 0:
                sent_a, kept_a, sent_b, kept_b = halved(kept, other, step)
                with jax.named_scope(f"{scope}{step}"):
                    other = [
                        flip(sent, orders[i][step - 1]) for i, sent in enumerate((sent_a, sent_b))
                    ]
                kept = [kept_a, kept_b]
                step -= 1
            messages = address(kept, other)
            with jax.named_scope(scope + "z"):
                return [messages[0]] + [shift(messages[k], -k) for k in (1, 2, 3)]

        def restored(arrived, scope, by_kind):
            mine = spread(by_tower(arrived), scope + "out")
            with jax.named_scope(scope + "out_core"):
                other = flip(mine, 1)
            return widen(mine, other, by_kind)

        grad_outer = [matmul_left(activated[k], d2).astype(low) for k in range(4)]
        outer_parts = cores(split_slots(grad_outer), "rs2_")
        grad_inner_pre = [
            (matmul_right(d2, w_out[k]) * gelu_slope(inner_pre[k])).astype(low) for k in range(4)
        ]
        grad_inner = [matmul_left(hidden, grad_inner_pre[k]).astype(low) for k in range(4)]
        inner_parts = cores(split_slots(grad_inner), "rs1_")
        grad_inner_bias = [jnp.sum(grad_inner_pre[k], 0, dtype=jnp.float32) for k in range(4)]
        query_out, passage_out = from_rows(result, "rows_o")
        grad_hidden1 = (
            sum(matmul_right(grad_inner_pre[k], w_in[k]) for k in range(4)) + grad_resid2
        )
        grad_gain1 = jnp.sum(grad_hidden1 * normed1, 0)
        grad_bias1 = jnp.sum(grad_hidden1, 0)
        grad_resid1 = norm_back(grad_hidden1, normed1, inverse1, gain1)
        grad_out_bias = jnp.sum(grad_resid1, 0)
        d1 = grad_resid1.astype(low)
        grad_out = matmul_left(attended, d1).astype(low)
        grad_attended = matmul_right(d1, w_o).astype(low)
        outer_z = reduced(*outer_parts, "rs2_")
        inner_z = reduced(*inner_parts, "rs1_")
        grad_query, grad_key, grad_value = attend_back(
            queries, key_vecs, value_vecs, grad_attended, log_total, labels
        )
        grad_kinds = [
            matmul_left(grad_query, tokens).astype(low),
            matmul_left(grad_key, tokens).astype(low),
            matmul_left(grad_value, tokens).astype(low),
            grad_out,
        ]
        attn_parts = cores(split_kinds(grad_kinds), "rs0_")
        grad_in = (
            matmul(grad_query, w_q) + matmul(grad_key, w_k) + matmul(grad_value, w_v) + grad_resid1
        ).astype(low)
        query_grad_in, passage_grad_in = from_rows(grad_in, "rows_g")
        attn_z = reduced(*attn_parts, "rs0_")
        full_outer = restored(outer_z, "rs2_", False)
        full_inner = restored(inner_z, "rs1_", False)
        full_attn = restored(attn_z, "rs0_", True).reshape(4, 2, 192, D)

        columns = lambda g: jnp.sum(g, 0, dtype=jnp.float32).reshape(4, 192)
        by_shard = turned(
            jnp.concatenate(
                [columns(grad_query), columns(grad_value), jnp.stack(grad_inner_bias, 0)], 1
            )
        )
        vectors = jnp.concatenate(
            [
                by_shard.reshape(6, D),
                jnp.stack(
                    [
                        grad_out_bias,
                        grad_gain1,
                        grad_bias1,
                        grad_outer_bias,
                        grad_gain2,
                        grad_bias2,
                    ],
                    0,
                ),
            ],
            0,
        )
        for step, bit in enumerate(orders[0]):
            with jax.named_scope(f"vec{step}"):
                vectors = vectors + flip(vectors, bit)
        picked = (cls_pos[:, None] == jnp.arange(512, dtype=jnp.int32)[None, :]).astype(low)
        vectors = jnp.concatenate([vectors, matmul(picked, result)], 0)
        with jax.named_scope("vec_z"):
            vectors = swap(jnp.broadcast_to(vectors[None], (4, 28, D)))
        mine_columns = vectors[:, 12:].astype(low).reshape(4, 16, 4, 192)
        zero = jnp.uint32(0)
        mine_columns = lax.dynamic_slice(
            mine_columns, (zero, zero, at, zero), (4, 16, 1, 192)
        ).reshape(4, 16, 192)
        query_pooled = mine_columns[QUERY_AT][None]
        passage_pooled = jnp.stack([mine_columns[n, :4] for n in (0, 1, 3)], 0)
        vectors = jnp.stack(
            [vectors[QUERY_AT, :12], vectors[0, :12] + vectors[1, :12] + vectors[3, :12]], 0
        )
        here = lax.dynamic_slice(
            vectors[:, :6].reshape(2, 4, 1152), (zero, at, zero), (2, 1, 1152)
        ).reshape(2, 1152)
        return (
            query_out,
            passage_out,
            query_grad_in,
            passage_grad_in,
            query_pooled,
            passage_pooled,
            turn(full_attn[0]),
            here[:, :192],
            turn(full_attn[1]),
            turn(full_attn[2]),
            here[:, 192:384],
            full_attn[3],
            vectors[:, 6],
            vectors[:, 7],
            vectors[:, 8],
            full_inner.reshape(2, D, D),
            here[:, 384:],
            full_outer.reshape(2, D, D),
            vectors[:, 9],
            vectors[:, 10],
            vectors[:, 11],
        )

    return per_device


def solution(mesh):
    rows = P(("wide", "narrow"), None)
    by_wide = P("wide", None)
    cols = P(None, None, "narrow")
    mids = P(None, "narrow", None)
    flat = P(None, "narrow")
    weights = (cols, flat, cols, cols, flat, mids, P(), P(), P(), cols, flat, mids, P(), P(), P())
    return jax.shard_map(
        build(mesh.shape["wide"]),
        mesh=mesh,
        in_specs=(rows,) * 4 + (by_wide,) * 4 + weights,
        out_specs=(rows,) * 4 + (P("wide", None, "narrow"),) * 2 + weights,
        check_vma=False,
    )
```
